32 devices in a mesh: groups: 2 (over x), tm: 16 (over z, y, core).
Axes of the slice: x: 2, y: 2, z: 4, core: 2. Of those that a mesh axis runs over, the one named last changes fastest.
Arguments:
- token_ids: int32 [4096, 8], P(('groups', 'tm')), parts along dimension 0, may hold values from 0 to 127
- field_offsets: int32 [16], P('groups'), parts along dimension 0, may hold values from 0 to 896
- embed_table: bfloat16 [1024, 1024], replicated, may hold values from -2.09375 to 2.09375
- w_in: bfloat16 [1024, 3072], P('tm'), may hold values from -0.1875 to 0.1875
- short_taps: float32 [3, 3072], replicated, may hold values from -1 to 1
- filters: bfloat16 [2, 1024, 2048], P(None, 'tm'), may hold values from -1.1 to 1.1
- cotangent: bfloat16 [4096, 1024], P(('groups', 'tm')), parts along dimension 0, may hold values from -0.125 to 0.125
Outputs:
- mixer_out: bfloat16 [4096, 1024], P(('groups', 'tm')), parts along dimension 0
- weight_grads: float32 [2048, 3072], P(('groups', 'tm')), parts along dimension 0
- tap_grads: float32 [6, 3072], P('groups'), parts along dimension 0
- filter_grads: float32 [4, 1024, 2048], P('groups', 'tm'), parts along dimension 0
The draws below stay inside these ranges and needn't reach their ends.
There are 2 independent parts, one for each index of `groups`. The reference program is written for one: setup_inputs(seed, part) draws one part's arguments, and reference() takes and returns one part's arrays. A program takes and returns all parts, laid end to end along the dimension named above; an argument that names none is the same for every part. Nothing has to cross between parts.
All inputs are finite; a program needn't handle non-finite values.
Results may differ from the reference program's by a relative error of at most 0.035.
Values may be sent and summed in bfloat16 or wider, within the bound.
A program may use at most 128 MiB of HBM per device.

```python
import jax
import jax.numpy as jnp

D = 1024
S = 8
K = 128
V = 1024
TOKENS = 2048


def draw_filters(key, part):
    key_rate, key_noise = jax.random.split(key)
    length = TOKENS
    low = jnp.log(0.25 / length)
    high = jnp.log(1.0 / 30.0)
    rate = jnp.exp(jax.random.uniform(key_rate, (2, D, 1), jnp.float32, low, high))
    lag = jnp.arange(length, dtype=jnp.float32)[None, None, :]
    envelope = jnp.sqrt(2.0 * rate) * jnp.exp(-rate * lag)
    noise = jnp.clip(jax.random.normal(key_noise, (2, D, length), jnp.float32), -4.0, 4.0)
    return (envelope * noise).astype(jnp.bfloat16)


def with_ends(array, stream_key, smallest, high):
    longest = array.shape.index(max(array.shape))
    spots = []
    for shift in (0, 1):
        where = [jax.random.randint(jax.random.fold_in(stream_key, axis), (), 0, length) for axis, length in enumerate(array.shape)]
        where[longest] = (where[longest] + shift) % array.shape[longest]
        spots.append(tuple(where))
    return array.at[spots[0]].set(smallest).at[spots[1]].set(high)


def levels(key, shape, cuts, smallest, largest):
    factor_of, own = 1.0, jax.random.fold_in(key, 6)
    for position, blocks in cuts:
        steps = jnp.exp(jax.random.uniform(jax.random.fold_in(own, position), (blocks,), jnp.float32, smallest / len(cuts), largest / len(cuts)))
        factor_of = factor_of * jnp.repeat(steps, shape[position] // blocks).reshape([-1 if axis == position else 1 for axis in range(len(shape))])
    return factor_of


def gaussian(rng, dims, width, limit, shards=(), kind=jnp.bfloat16):
    array = jax.random.normal(rng, dims, jnp.float32) * width
    if len(shards) > 0:
        array = levels(rng, dims, shards, -0.22, 0.18) * array
    return jnp.clip(array, min=-limit, max=limit).astype(kind)


def setup_inputs(seed: int = 0, part: int = 0) -> dict:
    splits = jax.random.split(jax.random.key(seed), 8)
    part_keys = jax.random.split(jax.random.fold_in(splits[7], part), 8)
    return {
        "token_ids": with_ends(jax.random.randint(part_keys[0], (TOKENS, S), 0, K), jax.random.fold_in(part_keys[0], 1), 0, K - 1).astype(jnp.int32),
        "field_offsets": with_ends(jax.random.randint(part_keys[1], (S,), 0, V - K + 1), jax.random.fold_in(part_keys[1], 1), 0, V - K).astype(jnp.int32),
        "embed_table": gaussian(splits[2], (V, D), 0.35, 2.09375),
        "w_in": gaussian(splits[3], (D, 3 * D), D ** -0.5, 0.1875, ((0, 16),)),
        "short_taps": jnp.clip(jax.random.uniform(splits[4], (3, 3 * D), jnp.float32, -1.0, 1.0), -1.0, 1.0),
        "filters": draw_filters(jax.random.fold_in(splits[7], 71), part),
        "cotangent": gaussian(part_keys[6], (TOKENS, D), (TOKENS ** -0.5), 0.125, ((0, 16),)),
    }


def reference(token_ids, field_offsets, embed_table, w_in, short_taps, filters, cotangent):
    row_index = (token_ids + field_offsets[None, :]).astype(jnp.int32)
    embedded = jnp.sum(jnp.take(embed_table, row_index, axis=0).astype(jnp.float32), axis=1).astype(jnp.bfloat16)
    proj = jnp.dot(embedded, w_in, preferred_element_type=jnp.float32).astype(jnp.bfloat16)
    length = proj.shape[0]
    total = 2 * length
    proj_wide = proj.astype(jnp.float32)
    padded = jnp.concatenate([jnp.zeros((2, proj.shape[1]), jnp.float32), proj_wide], axis=0)
    mixed = (short_taps[0] * padded[2:] + short_taps[1] * padded[1:length + 1] + short_taps[2] * padded[:length]).astype(jnp.bfloat16)
    values = mixed[:, :D].astype(jnp.float32)
    first_gate = mixed[:, D:2 * D].astype(jnp.float32)
    second_gate = mixed[:, 2 * D:].astype(jnp.float32)

    def spectrum(series):
        return jnp.fft.rfft(series.T, n=total, axis=-1)

    def signal(spec):
        return jnp.fft.irfft(spec, n=total, axis=-1)[:, :length]

    first_spec = jnp.fft.rfft(filters[0].astype(jnp.float32), n=total, axis=-1)
    second_spec = jnp.fft.rfft(filters[1].astype(jnp.float32), n=total, axis=-1)
    value_spec = spectrum(values)
    first_conv = signal(value_spec * first_spec).T.astype(jnp.bfloat16).astype(jnp.float32)
    first_mix = (first_gate * first_conv).astype(jnp.bfloat16).astype(jnp.float32)
    mix_spec = spectrum(first_mix)
    second_conv = signal(mix_spec * second_spec).T.astype(jnp.bfloat16).astype(jnp.float32)
    mixer_out = (second_gate * second_conv).astype(jnp.bfloat16)
    upstream = cotangent.astype(jnp.float32)
    grad_conv2 = (upstream * second_gate).astype(jnp.bfloat16).astype(jnp.float32)
    grad_gate2 = (upstream * second_conv).astype(jnp.bfloat16)
    grad_spec2 = spectrum(grad_conv2)
    grad_mix = signal(grad_spec2 * jnp.conj(second_spec)).T.astype(jnp.bfloat16).astype(jnp.float32)
    filter_two = signal(grad_spec2 * jnp.conj(mix_spec))
    grad_gate1 = (grad_mix * first_conv).astype(jnp.bfloat16)
    grad_conv1 = (grad_mix * first_gate).astype(jnp.bfloat16).astype(jnp.float32)
    grad_spec1 = spectrum(grad_conv1)
    grad_values = signal(grad_spec1 * jnp.conj(first_spec)).T.astype(jnp.bfloat16)
    filter_one = signal(grad_spec1 * jnp.conj(value_spec))
    filter_grads = jnp.stack([filter_one, filter_two], axis=0)
    grad_mixed = jnp.concatenate([grad_values, grad_gate1, grad_gate2], axis=1).astype(jnp.float32)
    grad_padded = jnp.concatenate([grad_mixed, jnp.zeros((2, grad_mixed.shape[1]), jnp.float32)], axis=0)
    grad_proj = (short_taps[0] * grad_mixed + short_taps[1] * grad_padded[1:length + 1] + short_taps[2] * grad_padded[2:]).astype(jnp.bfloat16)
    tap_grads = jnp.stack([
        jnp.sum(grad_mixed * padded[2:], axis=0),
        jnp.sum(grad_mixed * padded[1:length + 1], axis=0),
        jnp.sum(grad_mixed * padded[:length], axis=0)], axis=0)
    weight_grads = jnp.dot(embedded.T, grad_proj, preferred_element_type=jnp.float32)
    return mixer_out, weight_grads, tap_grads, filter_grads
```

```python
import math

import jax
import jax.numpy as jnp
from jax import lax
from jax.sharding import PartitionSpec as P

DENSE_LIMIT = 4096


def widen(array):
    return array.astype(jnp.float32)


def narrow(array):
    return array.astype(jnp.bfloat16)


def dense_table(total):
    half = total // 2
    inner = 1 << (total.bit_length() - 1) // 2
    outer = half // inner
    step = lax.optimization_barrier(jnp.arange(half, dtype=jnp.int32))
    unit = 2.0 * math.pi / total

    def cis(count, stride):
        index = jnp.arange(count, dtype=jnp.int32)[:, None] * stride * step[None, :] % total
        angle = unit * index.astype(jnp.float32)
        return (jnp.cos(angle), jnp.sin(angle))

    coarse_cos, coarse_sin = cis(outer, inner)
    fine_cos, fine_sin = cis(inner, 1)
    left = jnp.stack([coarse_cos, -coarse_sin])[:, :, None, :]
    right = jnp.stack([-coarse_sin, -coarse_cos])[:, :, None, :]
    table = (left * fine_cos + right * fine_sin).reshape(total, half)
    row = lax.broadcasted_iota(jnp.int32, (total, half), 0)
    parity = (1 - 2 * (step % 2)).astype(jnp.float32)
    return narrow(jnp.where(row == half, parity[None, :], table))


class Dense:
    def __init__(self, total):
        self.half = total // 2
        self.table = dense_table(total)
        first = lax.broadcasted_iota(jnp.int32, (1, self.half), 1) == 0
        self.first = first
        self.scale = jnp.where(first, 1.0 / total, 2.0 / total).astype(jnp.float32)

    def spectrum(self, series):
        both = lax.dot_general(
            series, self.table, (((1,), (1,)), ((), ())), preferred_element_type=jnp.float32
        )
        return (both[:, : self.half], both[:, self.half :])

    def product(self, left, right, conjugate):
        left_re, left_im = left
        right_re, right_im = right
        across = left_im * right_im
        if conjugate:
            real = left_re * right_re + jnp.where(self.first, 0.0, across)
            imag = left_im * right_re - left_re * right_im
        else:
            real = left_re * right_re - jnp.where(self.first, 0.0, across)
            imag = left_re * right_im + left_im * right_re
        imag = jnp.where(self.first, across, imag)
        return (real * self.scale, imag * self.scale)

    def signal(self, pair):
        joined = narrow(jnp.concatenate(pair, axis=1))
        return jnp.dot(joined, self.table, preferred_element_type=jnp.float32)


def cis_tables(count_a, count_b, modulus):
    left = jnp.arange(count_a, dtype=jnp.int32)[:, None]
    right = jnp.arange(count_b, dtype=jnp.int32)[None, :]
    angle = 2.0 * math.pi / modulus * (left * right % modulus).astype(jnp.float32)
    return (jnp.cos(angle), jnp.sin(angle))


class Factored:
    def __init__(self, total):
        bits = total.bit_length() - 1
        first_len = 1 << (bits + 1) // 2
        second_len = total // first_len
        first_cos, first_sin = cis_tables(first_len, first_len // 2, first_len)
        second_cos, second_sin = cis_tables(second_len, second_len, second_len)
        self.total = total
        self.second_len = second_len
        self.twist_cos, self.twist_sin = cis_tables(first_len, second_len, total)
        self.first_both = jnp.concatenate([first_cos, -first_sin], axis=0)
        self.forward = jnp.block([[second_cos, -second_sin], [second_sin, second_cos]])
        self.inverse = jnp.block([[second_cos, second_sin], [-second_sin, second_cos]])

    def spectrum(self, series):
        series = widen(series)
        channels, length = series.shape
        rows_k = self.twist_cos.shape[0]
        half = self.first_both.shape[1]
        blocks = series.reshape(channels, half, length // half)
        part = jnp.einsum("ka,cab->ckb", self.first_both, blocks)
        part_re = part[:, :rows_k]
        part_im = part[:, rows_k:]
        turn_re = part_re * self.twist_cos + part_im * self.twist_sin
        turn_im = part_im * self.twist_cos - part_re * self.twist_sin
        turned = jnp.concatenate([turn_re, turn_im], axis=2)
        result = jnp.einsum("ckb,bm->ckm", turned, self.forward)
        return (result[:, :, : self.second_len], result[:, :, self.second_len :])

    def product(self, left, right, conjugate):
        left_re, left_im = left
        right_re, right_im = right
        if conjugate:
            right_im = -right_im
        return (left_re * right_re - left_im * right_im, left_re * right_im + left_im * right_re)

    def signal(self, pair):
        joined = jnp.concatenate(pair, axis=2)
        back = jnp.einsum("ckm,mb->ckb", joined, self.inverse)
        back_re = back[:, :, : self.second_len]
        back_im = back[:, :, self.second_len :]
        turn_re = back_re * self.twist_cos - back_im * self.twist_sin
        turn_im = back_im * self.twist_cos + back_re * self.twist_sin
        turned = jnp.concatenate([turn_re, turn_im], axis=1)
        blocks = jnp.einsum("ka,ckb->cab", self.first_both, turned)
        return blocks.reshape(joined.shape[0], -1) * (1.0 / self.total)


def delayed(array, steps):
    length = array.shape[1]
    return jnp.pad(array, ((0, 0), (steps, 0)))[:, :length]


def advanced(array, steps):
    return jnp.pad(array, ((0, 0), (0, steps)))[:, steps:]


def local(token_ids, field_offsets, embed_table, w_in, short_taps, filters, cotangent):
    rows, width = cotangent.shape
    fields = token_ids.shape[1]
    peers = lax.axis_size("tm")
    me = lax.axis_index("tm")
    chans = width // peers
    length = rows * peers
    vocab = embed_table.shape[0]

    w_part = w_in.reshape(chans, 3, peers, chans).transpose(2, 0, 1, 3).reshape(peers, chans, 3 * chans)
    cot_part = cotangent.reshape(rows, peers, chans).transpose(1, 2, 0)
    tok_part = narrow(token_ids).T.reshape(1, chans, -1)
    tok_part = jnp.broadcast_to(tok_part, (peers,) + tok_part.shape[1:])
    sent = jnp.concatenate([w_part, cot_part, tok_part], axis=2)
    got = lax.all_to_all(sent, "tm", split_axis=0, concat_axis=0, tiled=True)
    w_own = got[:, :, : 3 * chans].reshape(width, 3 * chans)
    upstream = widen(got[:, :, 3 * chans : 3 * chans + rows].transpose(1, 0, 2).reshape(chans, length))
    tokens = got[:, :, 3 * chans + rows :].reshape(peers, fields, rows)
    tokens = tokens.transpose(1, 0, 2).reshape(fields, length).astype(jnp.int32)
    row_index = tokens + field_offsets[:, None]

    codes = lax.broadcasted_iota(jnp.int32, (vocab, length), 0)
    counts = jnp.zeros((vocab, length), jnp.float32)
    for field in range(fields):
        counts = counts + jnp.where(codes == row_index[field][None, :], 1.0, 0.0)
    embedded = narrow(
        jnp.einsum("vr,vt->rt", embed_table, narrow(counts), preferred_element_type=jnp.float32)
    )
    proj = narrow(jnp.einsum("rc,rt->ct", w_own, embedded, preferred_element_type=jnp.float32))
    taps = lax.dynamic_index_in_dim(short_taps.reshape(3, 3, peers, chans), me, 2, keepdims=False)
    taps = taps.reshape(3, 3 * chans, 1)
    proj_wide = widen(proj)
    lags = (proj_wide, delayed(proj_wide, 1), delayed(proj_wide, 2))
    mixed = narrow(taps[0] * lags[0] + taps[1] * lags[1] + taps[2] * lags[2])
    values = mixed[:chans]
    first_gate = widen(mixed[chans : 2 * chans])
    second_gate = widen(mixed[2 * chans :])

    transform = (Dense if 2 * length <= DENSE_LIMIT else Factored)(2 * length)

    def spectra(*series):
        whole = transform.spectrum(jnp.concatenate(series, axis=0))
        return [
            tuple(part[i * chans : (i + 1) * chans] for part in whole) for i in range(len(series))
        ]

    def signals(*pairs):
        whole = transform.signal(tuple(jnp.concatenate(parts, axis=0) for parts in zip(*pairs)))
        return [whole[i * chans : (i + 1) * chans] for i in range(len(pairs))]

    grad_conv2 = narrow(upstream * second_gate)
    first_spec, second_spec, value_spec, grad_spec2 = spectra(
        filters[0], filters[1], values, grad_conv2
    )
    first_conv, grad_mix = signals(
        transform.product(value_spec, first_spec, False),
        transform.product(grad_spec2, second_spec, True),
    )
    first_conv = widen(narrow(first_conv))
    grad_mix = widen(narrow(grad_mix))
    first_mix = narrow(first_gate * first_conv)
    grad_gate1 = narrow(grad_mix * first_conv)
    grad_conv1 = narrow(grad_mix * first_gate)
    mix_spec, grad_spec1 = spectra(first_mix, grad_conv1)
    second_conv, grad_values, filter_one, filter_two = signals(
        transform.product(mix_spec, second_spec, False),
        transform.product(grad_spec1, first_spec, True),
        transform.product(grad_spec1, value_spec, True),
        transform.product(grad_spec2, mix_spec, True),
    )
    second_conv = widen(narrow(second_conv))
    mixer_out = narrow(second_gate * second_conv)
    grad_gate2 = narrow(upstream * second_conv)
    filter_grads = jnp.stack([filter_one, filter_two], axis=0)
    grad_mixed = jnp.concatenate([narrow(grad_values), grad_gate1, grad_gate2], axis=0)
    grad_wide = widen(grad_mixed)
    grad_proj = narrow(
        taps[0] * grad_wide + taps[1] * advanced(grad_wide, 1) + taps[2] * advanced(grad_wide, 2)
    )
    tap_terms = jnp.stack([jnp.sum(grad_wide * lag, axis=1) for lag in lags], axis=0)
    weight_terms = narrow(
        jnp.einsum("rt,ct->rc", embedded, grad_proj, preferred_element_type=jnp.float32)
    )

    weight_part = weight_terms.reshape(peers, chans, 3 * chans)
    mixer_part = mixer_out.reshape(chans, peers, rows).transpose(1, 0, 2)
    tap_part = narrow(tap_terms).reshape(1, chans, -1)
    tap_part = jnp.broadcast_to(tap_part, (peers,) + tap_part.shape[1:])
    back = lax.all_to_all(
        jnp.concatenate([weight_part, mixer_part, tap_part], axis=2),
        "tm",
        split_axis=0,
        concat_axis=0,
        tiled=True,
    )
    weight_grads = widen(
        back[:, :, : 3 * chans].reshape(peers, chans, 3, chans).transpose(1, 2, 0, 3)
    ).reshape(chans, 3 * width)
    mixer_rows = back[:, :, 3 * chans : 3 * chans + rows].reshape(width, rows).T
    tap_grads = widen(
        back[:, :, 3 * chans + rows :].reshape(peers, 3, 3, chans).transpose(1, 2, 0, 3)
    ).reshape(3, 3 * width)
    return (mixer_rows, weight_grads, tap_grads, filter_grads)


def solution(mesh):
    return jax.shard_map(
        local,
        mesh=mesh,
        in_specs=(
            P(("groups", "tm"), None),
            P("groups"),
            P(),
            P("tm", None),
            P(),
            P(None, "tm", None),
            P(("groups", "tm"), None),
        ),
        out_specs=(
            P(("groups", "tm"), None),
            P(("groups", "tm"), None),
            P("groups", None),
            P("groups", "tm", None),
        ),
        check_vma=False,
    )
```

```python
import math

import jax
import jax.numpy as jnp
from jax import lax
from jax.experimental import pallas as pl
from jax.experimental.pallas import tpu as pltpu
from jax.sharding import PartitionSpec as P

DENSE_LIMIT = 4096
CODES = 128
CHUNK = 512
VMEM = 56 << 20


def widen(array):
    return array.astype(jnp.float32)


def narrow(array):
    return array.astype(jnp.bfloat16)


def dense_table(total):
    half = total // 2
    inner = 1 << (total.bit_length() - 1) // 2
    outer = half // inner
    step = lax.optimization_barrier(jnp.arange(half, dtype=jnp.int32))
    unit = 2.0 * math.pi / total

    def cis(count, stride):
        index = jnp.arange(count, dtype=jnp.int32)[:, None] * stride * step[None, :] % total
        angle = unit * index.astype(jnp.float32)
        return (jnp.cos(angle), jnp.sin(angle))

    coarse_cos, coarse_sin = cis(outer, inner)
    fine_cos, fine_sin = cis(inner, 1)
    left = jnp.stack([coarse_cos, -coarse_sin])[:, :, None, :]
    right = jnp.stack([-coarse_sin, -coarse_cos])[:, :, None, :]
    return narrow(left * fine_cos + right * fine_sin).reshape(2, half, half)


def spread(rows, columns, start):
    row = lax.broadcasted_iota(jnp.int32, (rows, columns), 0) + start
    return 1.0 - 2.0 * (row & 1).astype(jnp.float32)


def mixer_kernel(
    table_hbm, signals, gates, convs, gate_grad, filter_grads, table, spec_re, spec_im, prod_re, prod_im, stage, sems
):
    half, pair = gates.shape
    chans = pair // 2
    total = 2 * half
    chunk = min(CHUNK, half)
    steps = half // chunk

    def copy(part, step):
        rows = pl.ds(pl.multiple_of(step * chunk, chunk), chunk)
        return pltpu.make_async_copy(
            table_hbm.at[part, rows], table.at[part, rows], sems.at[part, step]
        )

    for step in range(steps):
        copy(0, step).start()
        copy(1, step).start()

    def window(step):
        return pl.ds(pl.multiple_of(step * chunk, chunk), chunk)

    def dot(left, right):
        return jnp.dot(left, right, preferred_element_type=jnp.float32)

    parity = 1 - 2 * (lax.broadcasted_iota(jnp.int32, (16, half), 1) & 1)
    parity = parity.astype(jnp.float32).astype(jnp.bfloat16)
    lane = lax.broadcasted_iota(jnp.int32, (1, pair), 1)
    early = lane < chans
    sign = jnp.where(early, 1.0, -1.0)

    def scales(step):
        row = lax.broadcasted_iota(jnp.int32, (chunk, pair), 0) + step * chunk
        return jnp.where(row == 0, 1.0 / total, 2.0 / total)

    def swap(value):
        return pltpu.roll(value, chans, 1)

    alternating = dot(parity, signals[...])[:1]
    ends_filter = alternating[:, :pair]
    ends_value = alternating[:, pair:]

    def first(step, carry):
        rows = window(step)
        copy(0, step).wait()
        spec_re[rows, :] = dot(table[0, rows, :], signals[...])
        copy(1, step).wait()
        spec_im[rows, :] = dot(table[1, rows, :], signals[...])
        other_re, other_im = spec_re[rows, :pair], spec_im[rows, :pair]
        real, imag = spec_re[rows, pair:], spec_im[rows, pair:]
        scale = scales(step)
        prod_re[rows, :pair] = narrow((real * other_re - sign * imag * other_im) * scale)
        prod_im[rows, :pair] = narrow((sign * real * other_im + imag * other_re) * scale)
        return carry

    lax.fori_loop(0, steps, first, 0)
    ends_first = ends_value * ends_filter * (1.0 / total)

    def second(step, carry):
        rows = window(step)
        out = dot(table[0, rows, :], prod_re[:, :pair]) + dot(table[1, rows, :], prod_im[:, :pair])
        out = out + spread(chunk, pair, step * chunk) * ends_first
        out = widen(narrow(out))
        stage[rows, :] = narrow(out * widen(gates[rows, :]))
        gate_grad[rows, :] = narrow(out * swap(out))
        return carry

    lax.fori_loop(0, steps, second, 0)
    ends_mix = dot(parity, stage[...])[:1]

    def third(step, carry):
        rows = window(step)
        mixed_re = dot(table[0, rows, :], stage[...])
        mixed_im = dot(table[1, rows, :], stage[...])
        filt_re, filt_im = swap(spec_re[rows, :pair]), swap(spec_im[rows, :pair])
        flip_re, flip_im = swap(spec_re[rows, pair:]), swap(spec_im[rows, pair:])
        left_re = jnp.where(early, flip_re, mixed_re)
        left_im = jnp.where(early, flip_im, mixed_im)
        right_re = jnp.where(early, mixed_re, flip_re)
        right_im = jnp.where(early, mixed_im, flip_im)
        scale = scales(step)
        prod_re[rows, :pair] = narrow((mixed_re * filt_re - sign * mixed_im * filt_im) * scale)
        prod_im[rows, :pair] = narrow((sign * mixed_re * filt_im + mixed_im * filt_re) * scale)
        prod_re[rows, pair:] = narrow((left_re * right_re + left_im * right_im) * scale)
        prod_im[rows, pair:] = narrow((left_im * right_re - left_re * right_im) * scale)
        return carry

    lax.fori_loop(0, steps, third, 0)
    ends_conv = ends_mix * swap(jnp.broadcast_to(ends_filter, (8, pair)))[:1] * (1.0 / total)
    flip = swap(jnp.broadcast_to(ends_value, (8, pair)))[:1]
    ends_lag = ends_mix * flip * (1.0 / total)

    def fourth(step, carry):
        rows = window(step)
        out = dot(table[0, rows, :], prod_re[...]) + dot(table[1, rows, :], prod_im[...])
        weave = spread(chunk, pair, step * chunk)
        convs[rows, :] = narrow(out[:, :pair] + weave * ends_conv)
        lagged = (out[:, pair:] + weave * ends_lag).T
        filter_grads[1, :, rows] = lagged[:chans]
        filter_grads[0, :, rows] = lagged[chans:]
        return carry

    lax.fori_loop(0, steps, fourth, 0)


def fused_mixer(table, signals, gates):
    half, pair = gates.shape
    chans = pair // 2
    steps = half // min(CHUNK, half)
    whole = pl.BlockSpec(memory_space=pltpu.VMEM)
    wide = pltpu.VMEM((half, 2 * pair), jnp.float32)
    packed = pltpu.VMEM((half, 2 * pair), jnp.bfloat16)
    flops = 2 * 2 * half * half * 2 * pair * 4
    return pl.pallas_call(
        mixer_kernel,
        out_shape=(
            jax.ShapeDtypeStruct((half, pair), jnp.bfloat16),
            jax.ShapeDtypeStruct((half, pair), jnp.bfloat16),
            jax.ShapeDtypeStruct((2, chans, half), jnp.float32),
        ),
        in_specs=[pl.BlockSpec(memory_space=pl.ANY), whole, whole],
        out_specs=(whole, whole, whole),
        scratch_shapes=[
            pltpu.VMEM((2, half, half), jnp.bfloat16),
            wide,
            wide,
            packed,
            packed,
            pltpu.VMEM((half, pair), jnp.bfloat16),
            pltpu.SemaphoreType.DMA((2, steps)),
        ],
        compiler_params=pltpu.CompilerParams(vmem_limit_bytes=VMEM),
        cost_estimate=pl.CostEstimate(
            flops=flops, bytes_accessed=4 * half * half, transcendentals=0
        ),
        name="mixer",
    )(table, signals, gates)


def pack_kernel(w_ref, cot_ref, tok_ref, out_ref):
    peers, chans, _ = out_ref.shape
    rows, width = cot_ref.shape
    tok = tok_ref[...]
    for peer in range(peers):
        own = slice(peer * chans, (peer + 1) * chans)
        pieces = [w_ref[:, j * width + peer * chans : j * width + (peer + 1) * chans] for j in range(3)]
        pieces += [cot_ref[:chans, own], cot_ref[chans:, own], tok[:chans], tok[chans:]]
        out_ref[peer] = jnp.concatenate(pieces, axis=1)


def unpack_kernel(got_ref, mixer_ref, weight_ref):
    peers, chans, _ = got_ref.shape
    width = peers * chans
    for peer in range(0, peers, 2):
        low, high = got_ref[peer], got_ref[peer + 1]
        for j in range(5):
            own = slice(j * chans, (j + 1) * chans)
            both = jnp.concatenate([low[:, own], high[:, own]], axis=1)
            if j < 3:
                start = j * width + peer * chans
                weight_ref[:, start : start + 2 * chans] = widen(both)
            else:
                top = (j - 3) * chans
                mixer_ref[top : top + chans, peer * chans : (peer + 2) * chans] = both


def local(token_ids, field_offsets, embed_table, w_in, short_taps, filters, cotangent):
    chans = cotangent.shape[1] // lax.axis_size("tm")
    dense = 2 * cotangent.shape[0] * lax.axis_size("tm") <= DENSE_LIMIT
    plan = fast_local if dense and chans == 64 and cotangent.shape[0] == 2 * chans else wide_local
    return plan(token_ids, field_offsets, embed_table, w_in, short_taps, filters, cotangent)


def later(array, steps):
    return jnp.pad(array, ((steps, 0), (0, 0)))[: array.shape[0]]


def earlier(array, steps):
    return jnp.pad(array, ((0, steps), (0, 0)))[steps:]


def fast_local(token_ids, field_offsets, embed_table, w_in, short_taps, filters, cotangent):
    rows, width = cotangent.shape
    fields = token_ids.shape[1]
    peers = lax.axis_size("tm")
    me = lax.axis_index("tm")
    chans = width // peers
    length = rows * peers
    lanes = 3 * chans + rows + 2 * fields
    sent = pl.pallas_call(
        pack_kernel,
        out_shape=jax.ShapeDtypeStruct((peers, chans, lanes), jnp.bfloat16),
        name="pack",
    )(w_in, cotangent, narrow(token_ids))
    got = lax.all_to_all(sent, "tm", split_axis=0, concat_axis=0, tiled=True)
    table = dense_table(2 * length)
    used = jnp.concatenate(
        [
            lax.dynamic_slice_in_dim(embed_table, field_offsets[field], CODES, 0)
            for field in range(fields)
        ],
        axis=0,
    )
    filter_rows = filters.transpose(2, 0, 1).reshape(length, 2 * chans)

    def halves(start, count):
        first = got[:, :, start : start + count]
        second = got[:, :, start + count : start + 2 * count]
        return jnp.concatenate([first, second], axis=1).reshape(length, count)

    w_own = got[:, :, : 3 * chans].reshape(width, 3 * chans)
    upstream = widen(halves(3 * chans, chans))
    tokens = halves(3 * chans + rows, fields)
    code = lax.broadcasted_iota(jnp.int32, (1, CODES), 1)
    code = narrow(code)
    chosen = jnp.concatenate(
        [narrow(tokens[:, field : field + 1] == code) for field in range(fields)], axis=1
    )
    embedded = narrow(jnp.dot(chosen, used, preferred_element_type=jnp.float32))
    proj = narrow(jnp.dot(embedded, w_own, preferred_element_type=jnp.float32))
    taps = lax.dynamic_index_in_dim(short_taps.reshape(3, 3, peers, chans), me, 2, keepdims=False)
    taps = taps.reshape(3, 1, 3 * chans)
    proj_wide = widen(proj)
    lags = (proj_wide, later(proj_wide, 1), later(proj_wide, 2))
    mixed = narrow(taps[0] * lags[0] + taps[1] * lags[1] + taps[2] * lags[2])
    values = mixed[:, :chans]
    first_gate = mixed[:, chans : 2 * chans]
    second_gate = widen(mixed[:, 2 * chans :])
    grad_conv2 = narrow(upstream * second_gate)
    convs, gate_grad, filter_grads = fused_mixer(
        table,
        jnp.concatenate([filter_rows, values, grad_conv2], axis=1),
        jnp.concatenate([first_gate, first_gate], axis=1),
    )
    second_conv = widen(convs[:, :chans])
    mixer_out = narrow(second_gate * second_conv)
    grad_gate2 = narrow(upstream * second_conv)
    grad_mixed = jnp.concatenate([convs[:, chans:], gate_grad[:, :chans], grad_gate2], axis=1)
    grad_wide = widen(grad_mixed)
    grad_proj = narrow(
        taps[0] * grad_wide + taps[1] * earlier(grad_wide, 1) + taps[2] * earlier(grad_wide, 2)
    )
    tap_terms = jnp.stack([jnp.sum(grad_wide * lag, axis=0) for lag in lags], axis=0)
    weight_terms = narrow(
        jnp.einsum("tr,tc->rc", embedded, grad_proj, preferred_element_type=jnp.float32)
    )
    mixer_part = mixer_out.reshape(peers, 2, chans, chans)
    tap_part = narrow(tap_terms).reshape(1, chans, -1)
    tap_part = jnp.broadcast_to(tap_part, (peers,) + tap_part.shape[1:])
    back = lax.all_to_all(
        jnp.concatenate(
            [weight_terms.reshape(peers, chans, -1), mixer_part[:, 0], mixer_part[:, 1], tap_part],
            axis=2,
        ),
        "tm",
        split_axis=0,
        concat_axis=0,
        tiled=True,
    )
    mixer_rows, weight_grads = pl.pallas_call(
        unpack_kernel,
        out_shape=(
            jax.ShapeDtypeStruct((rows, width), jnp.bfloat16),
            jax.ShapeDtypeStruct((chans, 3 * width), jnp.float32),
        ),
        name="unpack",
    )(back)
    tap_grads = widen(
        back[:, :, 3 * chans + rows :].reshape(peers, 3, 3, chans).transpose(1, 2, 0, 3)
    ).reshape(3, 3 * width)
    return (mixer_rows, weight_grads, tap_grads, filter_grads)


def cis_tables(count_a, count_b, modulus):
    left = jnp.arange(count_a, dtype=jnp.int32)[:, None]
    right = jnp.arange(count_b, dtype=jnp.int32)[None, :]
    angle = 2.0 * math.pi / modulus * (left * right % modulus).astype(jnp.float32)
    return (jnp.cos(angle), jnp.sin(angle))


class Factored:
    def __init__(self, total):
        bits = total.bit_length() - 1
        first_len = 1 << (bits + 1) // 2
        second_len = total // first_len
        first_cos, first_sin = cis_tables(first_len, first_len // 2, first_len)
        second_cos, second_sin = cis_tables(second_len, second_len, second_len)
        self.total = total
        self.second_len = second_len
        self.twist_cos, self.twist_sin = cis_tables(first_len, second_len, total)
        self.first_both = jnp.concatenate([first_cos, -first_sin], axis=0)
        self.forward = jnp.block([[second_cos, -second_sin], [second_sin, second_cos]])
        self.inverse = jnp.block([[second_cos, second_sin], [-second_sin, second_cos]])

    def spectrum(self, series):
        series = widen(series)
        channels, length = series.shape
        rows_k = self.twist_cos.shape[0]
        half = self.first_both.shape[1]
        blocks = series.reshape(channels, half, length // half)
        part = jnp.einsum("ka,cab->ckb", self.first_both, blocks)
        part_re = part[:, :rows_k]
        part_im = part[:, rows_k:]
        turn_re = part_re * self.twist_cos + part_im * self.twist_sin
        turn_im = part_im * self.twist_cos - part_re * self.twist_sin
        turned = jnp.concatenate([turn_re, turn_im], axis=2)
        result = jnp.einsum("ckb,bm->ckm", turned, self.forward)
        return (result[:, :, : self.second_len], result[:, :, self.second_len :])

    def product(self, left, right, conjugate):
        left_re, left_im = left
        right_re, right_im = right
        if conjugate:
            right_im = -right_im
        return (left_re * right_re - left_im * right_im, left_re * right_im + left_im * right_re)

    def signal(self, pair):
        joined = jnp.concatenate(pair, axis=2)
        back = jnp.einsum("ckm,mb->ckb", joined, self.inverse)
        back_re = back[:, :, : self.second_len]
        back_im = back[:, :, self.second_len :]
        turn_re = back_re * self.twist_cos - back_im * self.twist_sin
        turn_im = back_im * self.twist_cos + back_re * self.twist_sin
        turned = jnp.concatenate([turn_re, turn_im], axis=1)
        blocks = jnp.einsum("ka,ckb->cab", self.first_both, turned)
        return blocks.reshape(joined.shape[0], -1) * (1.0 / self.total)


def delayed(array, steps):
    length = array.shape[1]
    return jnp.pad(array, ((0, 0), (steps, 0)))[:, :length]


def advanced(array, steps):
    return jnp.pad(array, ((0, 0), (0, steps)))[:, steps:]


def wide_local(token_ids, field_offsets, embed_table, w_in, short_taps, filters, cotangent):
    rows, width = cotangent.shape
    fields = token_ids.shape[1]
    peers = lax.axis_size("tm")
    me = lax.axis_index("tm")
    chans = width // peers
    length = rows * peers
    vocab = embed_table.shape[0]

    w_part = w_in.reshape(chans, 3, peers, chans).transpose(2, 0, 1, 3).reshape(peers, chans, 3 * chans)
    cot_part = cotangent.reshape(rows, peers, chans).transpose(1, 2, 0)
    tok_part = narrow(token_ids).T.reshape(1, chans, -1)
    tok_part = jnp.broadcast_to(tok_part, (peers,) + tok_part.shape[1:])
    sent = jnp.concatenate([w_part, cot_part, tok_part], axis=2)
    got = lax.all_to_all(sent, "tm", split_axis=0, concat_axis=0, tiled=True)
    w_own = got[:, :, : 3 * chans].reshape(width, 3 * chans)
    upstream = widen(got[:, :, 3 * chans : 3 * chans + rows].transpose(1, 0, 2).reshape(chans, length))
    tokens = got[:, :, 3 * chans + rows :].reshape(peers, fields, rows)
    tokens = tokens.transpose(1, 0, 2).reshape(fields, length).astype(jnp.int32)
    row_index = tokens + field_offsets[:, None]

    codes = lax.broadcasted_iota(jnp.int32, (vocab, length), 0)
    counts = jnp.zeros((vocab, length), jnp.float32)
    for field in range(fields):
        counts = counts + jnp.where(codes == row_index[field][None, :], 1.0, 0.0)
    embedded = narrow(
        jnp.einsum("vr,vt->rt", embed_table, narrow(counts), preferred_element_type=jnp.float32)
    )
    proj = narrow(jnp.einsum("rc,rt->ct", w_own, embedded, preferred_element_type=jnp.float32))
    taps = lax.dynamic_index_in_dim(short_taps.reshape(3, 3, peers, chans), me, 2, keepdims=False)
    taps = taps.reshape(3, 3 * chans, 1)
    proj_wide = widen(proj)
    lags = (proj_wide, delayed(proj_wide, 1), delayed(proj_wide, 2))
    mixed = narrow(taps[0] * lags[0] + taps[1] * lags[1] + taps[2] * lags[2])
    values = mixed[:chans]
    first_gate = widen(mixed[chans : 2 * chans])
    second_gate = widen(mixed[2 * chans :])

    transform = Factored(2 * length)

    def spectra(*series):
        whole = transform.spectrum(jnp.concatenate(series, axis=0))
        return [
            tuple(part[i * chans : (i + 1) * chans] for part in whole) for i in range(len(series))
        ]

    def signals(*pairs):
        whole = transform.signal(tuple(jnp.concatenate(parts, axis=0) for parts in zip(*pairs)))
        return [whole[i * chans : (i + 1) * chans] for i in range(len(pairs))]

    grad_conv2 = narrow(upstream * second_gate)
    first_spec, second_spec, value_spec, grad_spec2 = spectra(
        filters[0], filters[1], values, grad_conv2
    )
    first_conv, grad_mix = signals(
        transform.product(value_spec, first_spec, False),
        transform.product(grad_spec2, second_spec, True),
    )
    first_conv = widen(narrow(first_conv))
    grad_mix = widen(narrow(grad_mix))
    first_mix = narrow(first_gate * first_conv)
    grad_gate1 = narrow(grad_mix * first_conv)
    grad_conv1 = narrow(grad_mix * first_gate)
    mix_spec, grad_spec1 = spectra(first_mix, grad_conv1)
    second_conv, grad_values, filter_one, filter_two = signals(
        transform.product(mix_spec, second_spec, False),
        transform.product(grad_spec1, first_spec, True),
        transform.product(grad_spec1, value_spec, True),
        transform.product(grad_spec2, mix_spec, True),
    )
    second_conv = widen(narrow(second_conv))
    mixer_out = narrow(second_gate * second_conv)
    grad_gate2 = narrow(upstream * second_conv)
    filter_grads = jnp.stack([filter_one, filter_two], axis=0)
    grad_mixed = jnp.concatenate([narrow(grad_values), grad_gate1, grad_gate2], axis=0)
    grad_wide = widen(grad_mixed)
    grad_proj = narrow(
        taps[0] * grad_wide + taps[1] * advanced(grad_wide, 1) + taps[2] * advanced(grad_wide, 2)
    )
    tap_terms = jnp.stack([jnp.sum(grad_wide * lag, axis=1) for lag in lags], axis=0)
    weight_terms = narrow(
        jnp.einsum("rt,ct->rc", embedded, grad_proj, preferred_element_type=jnp.float32)
    )

    weight_part = weight_terms.reshape(peers, chans, 3 * chans)
    mixer_part = mixer_out.reshape(chans, peers, rows).transpose(1, 0, 2)
    tap_part = narrow(tap_terms).reshape(1, chans, -1)
    tap_part = jnp.broadcast_to(tap_part, (peers,) + tap_part.shape[1:])
    back = lax.all_to_all(
        jnp.concatenate([weight_part, mixer_part, tap_part], axis=2),
        "tm",
        split_axis=0,
        concat_axis=0,
        tiled=True,
    )
    weight_grads = widen(
        back[:, :, : 3 * chans].reshape(peers, chans, 3, chans).transpose(1, 2, 0, 3)
    ).reshape(chans, 3 * width)
    mixer_rows = back[:, :, 3 * chans : 3 * chans + rows].reshape(width, rows).T
    tap_grads = widen(
        back[:, :, 3 * chans + rows :].reshape(peers, 3, 3, chans).transpose(1, 2, 0, 3)
    ).reshape(3, 3 * width)
    return (mixer_rows, weight_grads, tap_grads, filter_grads)


def solution(mesh):
    return jax.shard_map(
        local,
        mesh=mesh,
        in_specs=(
            P(("groups", "tm"), None),
            P("groups"),
            P(),
            P("tm", None),
            P(),
            P(None, "tm", None),
            P(("groups", "tm"), None),
        ),
        out_specs=(
            P(("groups", "tm"), None),
            P(("groups", "tm"), None),
            P("groups", None),
            P("groups", "tm", None),
        ),
        check_vma=False,
    )
```

```python
import math

import jax
import jax.numpy as jnp
from jax import lax
from jax.experimental import pallas as pl
from jax.experimental.pallas import tpu as pltpu
from jax.sharding import PartitionSpec as P

DENSE_LIMIT = 4096
CODES = 128
CHUNK = 512
VMEM = 56 << 20


def widen(array):
    return array.astype(jnp.float32)


def narrow(array):
    return array.astype(jnp.bfloat16)


def dense_table(total):
    half = total // 2
    inner = 1 << (total.bit_length() - 1) // 2
    outer = half // inner
    step = lax.optimization_barrier(jnp.arange(half, dtype=jnp.int32))
    unit = 2.0 * math.pi / total

    def cis(count, stride):
        index = jnp.arange(count, dtype=jnp.int32)[:, None] * stride * step[None, :] % total
        angle = unit * index.astype(jnp.float32)
        return (jnp.cos(angle), jnp.sin(angle))

    coarse_cos, coarse_sin = cis(outer, inner)
    fine_cos, fine_sin = cis(inner, 1)
    whole = pl.BlockSpec(memory_space=pltpu.VMEM)
    return pl.pallas_call(
        table_kernel,
        grid=(outer,),
        out_shape=jax.ShapeDtypeStruct((2, half, half), jnp.bfloat16),
        in_specs=[whole] * 4,
        out_specs=pl.BlockSpec((2, inner, half), lambda i: (0, i, 0)),
        cost_estimate=pl.CostEstimate(
            flops=6 * half * half, bytes_accessed=4 * half * half, transcendentals=0
        ),
        compiler_params=pltpu.CompilerParams(vmem_limit_bytes=24 << 20),
        name="table",
    )(coarse_cos, coarse_sin, fine_cos, fine_sin)


def table_kernel(coarse_cos, coarse_sin, fine_cos, fine_sin, out):
    row = pl.ds(pl.program_id(0), 1)
    high_cos, high_sin = coarse_cos[row, :], coarse_sin[row, :]
    low_cos, low_sin = fine_cos[...], fine_sin[...]
    out[0] = narrow(high_cos * low_cos - high_sin * low_sin)
    out[1] = narrow(-(high_sin * low_cos + high_cos * low_sin))


def embed_kernel(tokens, used, w_own, embedded, proj):
    picked = tokens[...]
    code = lax.broadcasted_iota(jnp.int32, (picked.shape[0], CODES), 1)
    chosen = [
        narrow(jnp.where(picked[:, field : field + 1] == code, 1.0, 0.0))
        for field in range(picked.shape[1])
    ]
    rows = narrow(
        jnp.dot(
            jnp.concatenate(chosen, axis=1), used[...], preferred_element_type=jnp.float32
        )
    )
    embedded[...] = rows
    proj[...] = narrow(jnp.dot(rows, w_own[...], preferred_element_type=jnp.float32))


def embed(tokens, used, w_own):
    length, fields = tokens.shape
    width, columns = w_own.shape
    block = 256
    whole = pl.BlockSpec(memory_space=pltpu.VMEM)
    return pl.pallas_call(
        embed_kernel,
        grid=(length // block,),
        out_shape=(
            jax.ShapeDtypeStruct((length, width), jnp.bfloat16),
            jax.ShapeDtypeStruct((length, columns), jnp.bfloat16),
        ),
        in_specs=[pl.BlockSpec((block, fields), lambda i: (i, 0)), whole, whole],
        out_specs=(
            pl.BlockSpec((block, width), lambda i: (i, 0)),
            pl.BlockSpec((block, columns), lambda i: (i, 0)),
        ),
        compiler_params=pltpu.CompilerParams(vmem_limit_bytes=24 << 20),
        name="embed",
    )(tokens, used, w_own)


def spread(rows, columns, start):
    row = lax.broadcasted_iota(jnp.int32, (rows, columns), 0) + start
    return 1.0 - 2.0 * (row & 1).astype(jnp.float32)


def dot(left, right):
    return jnp.dot(left, right, preferred_element_type=jnp.float32)


def quarter(rows, columns, start):
    turn = (lax.broadcasted_iota(jnp.int32, (rows, columns), 0) + start) & 3
    real = jnp.where(turn == 0, 1.0, jnp.where(turn == 2, -1.0, 0.0))
    imag = jnp.where(turn == 1, 1.0, jnp.where(turn == 3, -1.0, 0.0))
    return (real, imag)


def mixer_kernel(
    table_hbm, signals, gates, convs, gate_grad, lag_re, lag_im, ends, table, spec_re, spec_im, prod_re, prod_im, stage, sems
):
    half, pair = gates.shape
    middle = half // 2
    chans = pair // 2
    total = 2 * half
    chunk = min(CHUNK, middle)
    steps = half // chunk

    def window(step, base=0):
        return pl.ds(pl.multiple_of(step * chunk + base, chunk), chunk)

    def copy(part, step):
        rows = window(step)
        return pltpu.make_async_copy(
            table_hbm.at[part, rows], table.at[part, rows], sems.at[part, step]
        )

    for step in range(steps):
        copy(0, step).start()
        copy(1, step).start()

    parity = 1 - 2 * (lax.broadcasted_iota(jnp.int32, (16, half), 1) & 1)
    parity = parity.astype(jnp.float32).astype(jnp.bfloat16)
    early = lax.broadcasted_iota(jnp.int32, (1, pair), 1) < chans
    sign = jnp.where(early, 1.0, -1.0)

    def swap(value):
        return pltpu.roll(value, chans, 1)

    def keep(step, real, imag, to_re, to_im):
        rows = window(step)
        row = lax.broadcasted_iota(jnp.int32, (chunk, pair), 0) + step * chunk
        scale = jnp.where(row == 0, 1.0 / total, 2.0 / total)
        real, imag = real * scale, imag * scale
        cos, sin = quarter(chunk, pair, step * chunk)
        to_re[rows, :pair] = narrow(real)
        to_im[rows, :pair] = narrow(imag)
        to_re[rows, pair:] = narrow(cos * real - sin * imag)
        to_im[rows, pair:] = narrow(sin * real + cos * imag)

    alternating = dot(parity, signals[...])[:8]
    ends_filter = alternating[:, :pair]
    ends_value = alternating[:, pair:]

    def first(step, carry):
        rows = window(step)
        copy(0, step).wait()
        spec_re[rows, :] = dot(table[0, rows, :], signals[...])
        copy(1, step).wait()
        spec_im[rows, :] = dot(table[1, rows, :], signals[...])
        other_re, other_im = spec_re[rows, :pair], spec_im[rows, :pair]
        real, imag = spec_re[rows, pair:], spec_im[rows, pair:]
        keep(
            step,
            real * other_re - sign * imag * other_im,
            sign * real * other_im + imag * other_re,
            prod_re,
            prod_im,
        )
        return carry

    lax.fori_loop(0, steps, first, 0)
    ends_first = (ends_value * ends_filter * (1.0 / total))[:1]

    def second(step, carry):
        rows = window(step)
        both = dot(table[0, rows, :], prod_re[...]) + dot(table[1, rows, :], prod_im[...])
        weave = spread(chunk, pair, step * chunk) * ends_first
        for part in range(2):
            lanes = slice(part * pair, (part + 1) * pair)
            place = window(step, part * middle)
            out = widen(narrow(both[:, lanes] + weave))
            stage[rows, lanes] = narrow(out * widen(gates[place, :]))
            gate_grad[place, :] = narrow(out * swap(out))
        return carry

    lax.fori_loop(0, steps // 2, second, 0)
    ends_both = dot(parity[:, :middle], stage[...])[:8]
    ends_mix = ends_both[:, :pair] + ends_both[:, pair:]

    def third(step, carry):
        rows = window(step)
        half_re = dot(table[0, rows, :middle], stage[...])
        half_im = dot(table[1, rows, :middle], stage[...])
        cos, sin = quarter(chunk, pair, step * chunk)
        mixed_re = half_re[:, :pair] + cos * half_re[:, pair:] + sin * half_im[:, pair:]
        mixed_im = half_im[:, :pair] + cos * half_im[:, pair:] - sin * half_re[:, pair:]
        filt_re, filt_im = swap(spec_re[rows, :pair]), swap(spec_im[rows, :pair])
        flip_re, flip_im = swap(spec_re[rows, pair:]), swap(spec_im[rows, pair:])
        left_re = jnp.where(early, flip_re, mixed_re)
        left_im = jnp.where(early, flip_im, mixed_im)
        right_re = jnp.where(early, mixed_re, flip_re)
        right_im = jnp.where(early, mixed_im, flip_im)
        keep(
            step,
            mixed_re * filt_re - sign * mixed_im * filt_im,
            sign * mixed_re * filt_im + mixed_im * filt_re,
            prod_re,
            prod_im,
        )
        keep(
            step,
            left_re * right_re + left_im * right_im,
            left_im * right_re - left_re * right_im,
            lag_re,
            lag_im,
        )
        return carry

    lax.fori_loop(0, steps, third, 0)
    ends_conv = (ends_mix * swap(ends_filter) * (1.0 / total))[:1]
    ends[...] = ends_mix * swap(ends_value) * (1.0 / total)

    def fourth(step, carry):
        rows = window(step)
        both = dot(table[0, rows, :], prod_re[...]) + dot(table[1, rows, :], prod_im[...])
        weave = spread(chunk, pair, step * chunk) * ends_conv
        convs[rows, :] = narrow(both[:, :pair] + weave)
        convs[window(step, middle), :] = narrow(both[:, pair:] + weave)
        return carry

    lax.fori_loop(0, steps // 2, fourth, 0)


def lag_kernel(table_hbm, lag_re, lag_im, ends, filter_grads, table, sems):
    half, pair = lag_re.shape[0], lag_re.shape[1] // 2
    middle = half // 2
    chans = pair // 2
    chunk = min(CHUNK, middle)
    steps = middle // chunk

    def window(step, base=0):
        return pl.ds(pl.multiple_of(step * chunk + base, chunk), chunk)

    def copy(part, step):
        rows = window(step)
        return pltpu.make_async_copy(
            table_hbm.at[part, rows], table.at[part, rows], sems.at[part, step]
        )

    for step in range(steps):
        copy(0, step).start()
        copy(1, step).start()

    def body(step, carry):
        rows = window(step)
        copy(0, step).wait()
        copy(1, step).wait()
        both = dot(table[0, rows, :], lag_re[...]) + dot(table[1, rows, :], lag_im[...])
        weave = spread(chunk, pair, step * chunk) * ends[:1, :]
        for part in range(2):
            lagged = (both[:, part * pair : (part + 1) * pair] + weave).T
            place = window(step, part * middle)
            filter_grads[1, :, place] = lagged[:chans]
            filter_grads[0, :, place] = lagged[chans:]
        return carry

    lax.fori_loop(0, steps, body, 0)


def fused_mixer(table, signals, gates):
    half, pair = gates.shape
    steps = half // min(CHUNK, half // 2)
    whole = pl.BlockSpec(memory_space=pltpu.VMEM)
    wide = pltpu.VMEM((half, 2 * pair), jnp.float32)
    packed = pltpu.VMEM((half, 2 * pair), jnp.bfloat16)
    narrow_out = jax.ShapeDtypeStruct((half, pair), jnp.bfloat16)
    wide_out = jax.ShapeDtypeStruct((half, 2 * pair), jnp.bfloat16)
    return pl.pallas_call(
        mixer_kernel,
        out_shape=(
            narrow_out,
            narrow_out,
            wide_out,
            wide_out,
            jax.ShapeDtypeStruct((8, pair), jnp.float32),
        ),
        in_specs=[pl.BlockSpec(memory_space=pl.ANY), whole, whole],
        out_specs=(whole,) * 5,
        scratch_shapes=[
            pltpu.VMEM((2, half, half), jnp.bfloat16),
            wide,
            wide,
            packed,
            packed,
            pltpu.VMEM((half // 2, 2 * pair), jnp.bfloat16),
            pltpu.SemaphoreType.DMA((2, steps)),
        ],
        compiler_params=pltpu.CompilerParams(vmem_limit_bytes=VMEM),
        cost_estimate=pl.CostEstimate(
            flops=20 * half * half * pair, bytes_accessed=4 * half * half, transcendentals=0
        ),
        name="mixer",
    )(table, signals, gates)


def lag_grads(table, lag_re, lag_im, ends):
    half, pair = lag_re.shape[0], lag_re.shape[1] // 2
    middle = half // 2
    steps = middle // min(CHUNK, middle)
    whole = pl.BlockSpec(memory_space=pltpu.VMEM)
    return pl.pallas_call(
        lag_kernel,
        out_shape=jax.ShapeDtypeStruct((2, pair // 2, half), jnp.float32),
        in_specs=[pl.BlockSpec(memory_space=pl.ANY), whole, whole, whole],
        out_specs=whole,
        scratch_shapes=[
            pltpu.VMEM((2, middle, half), jnp.bfloat16),
            pltpu.SemaphoreType.DMA((2, steps)),
        ],
        compiler_params=pltpu.CompilerParams(vmem_limit_bytes=24 << 20),
        cost_estimate=pl.CostEstimate(
            flops=4 * half * half * pair, bytes_accessed=3 * half * half, transcendentals=0
        ),
        name="lags",
    )(table, lag_re, lag_im, ends)


def pack_kernel(w_ref, cot_ref, tok_ref, out_ref):
    peers, chans, _ = out_ref.shape
    rows, width = cot_ref.shape
    tok = tok_ref[...]
    for peer in range(peers):
        own = slice(peer * chans, (peer + 1) * chans)
        pieces = [w_ref[:, j * width + peer * chans : j * width + (peer + 1) * chans] for j in range(3)]
        pieces += [cot_ref[:chans, own], cot_ref[chans:, own], tok[:chans], tok[chans:]]
        out_ref[peer] = jnp.concatenate(pieces, axis=1)


def unpack_kernel(got_ref, mixer_ref, weight_ref):
    peers, chans, _ = got_ref.shape
    width = peers * chans
    for peer in range(0, peers, 2):
        low, high = got_ref[peer], got_ref[peer + 1]
        for j in range(5):
            own = slice(j * chans, (j + 1) * chans)
            both = jnp.concatenate([low[:, own], high[:, own]], axis=1)
            if j < 3:
                start = j * width + peer * chans
                weight_ref[:, start : start + 2 * chans] = widen(both)
            else:
                top = (j - 3) * chans
                mixer_ref[top : top + chans, peer * chans : (peer + 2) * chans] = both


def local(token_ids, field_offsets, embed_table, w_in, short_taps, filters, cotangent):
    chans = cotangent.shape[1] // lax.axis_size("tm")
    dense = 2 * cotangent.shape[0] * lax.axis_size("tm") <= DENSE_LIMIT
    plan = fast_local if dense and chans == 64 and cotangent.shape[0] == 2 * chans else wide_local
    return plan(token_ids, field_offsets, embed_table, w_in, short_taps, filters, cotangent)


def later(array, steps):
    return jnp.pad(array, ((steps, 0), (0, 0)))[: array.shape[0]]


def earlier(array, steps):
    return jnp.pad(array, ((0, steps), (0, 0)))[steps:]


def fast_local(token_ids, field_offsets, embed_table, w_in, short_taps, filters, cotangent):
    rows, width = cotangent.shape
    fields = token_ids.shape[1]
    peers = lax.axis_size("tm")
    me = lax.axis_index("tm")
    chans = width // peers
    length = rows * peers
    lanes = 3 * chans + rows + 2 * fields
    sent = pl.pallas_call(
        pack_kernel,
        out_shape=jax.ShapeDtypeStruct((peers, chans, lanes), jnp.bfloat16),
        name="pack",
    )(w_in, cotangent, narrow(token_ids))
    got = lax.all_to_all(sent, "tm", split_axis=0, concat_axis=0, tiled=True)
    table = dense_table(2 * length)
    used = jnp.concatenate(
        [
            lax.dynamic_slice_in_dim(embed_table, field_offsets[field], CODES, 0)
            for field in range(fields)
        ],
        axis=0,
    )
    filter_rows = filters.transpose(2, 0, 1).reshape(length, 2 * chans)

    def halves(start, count):
        first = got[:, :, start : start + count]
        second = got[:, :, start + count : start + 2 * count]
        return jnp.concatenate([first, second], axis=1).reshape(length, count)

    w_own = got[:, :, : 3 * chans].reshape(width, 3 * chans)
    upstream = widen(halves(3 * chans, chans))
    tokens = halves(3 * chans + rows, fields).astype(jnp.int32)
    embedded, proj = embed(tokens, used, w_own)
    taps = lax.dynamic_index_in_dim(short_taps.reshape(3, 3, peers, chans), me, 2, keepdims=False)
    taps = taps.reshape(3, 1, 3 * chans)
    proj_wide = widen(proj)
    lags = (proj_wide, later(proj_wide, 1), later(proj_wide, 2))
    mixed = narrow(taps[0] * lags[0] + taps[1] * lags[1] + taps[2] * lags[2])
    values = mixed[:, :chans]
    first_gate = mixed[:, chans : 2 * chans]
    second_gate = widen(mixed[:, 2 * chans :])
    grad_conv2 = narrow(upstream * second_gate)
    convs, gate_grad, lag_re, lag_im, ends = fused_mixer(
        table,
        jnp.concatenate([filter_rows, values, grad_conv2], axis=1),
        jnp.concatenate([first_gate, first_gate], axis=1),
    )
    second_conv = widen(convs[:, :chans])
    mixer_out = narrow(second_gate * second_conv)
    grad_gate2 = narrow(upstream * second_conv)
    grad_mixed = jnp.concatenate([convs[:, chans:], gate_grad[:, :chans], grad_gate2], axis=1)
    grad_wide = widen(grad_mixed)
    grad_proj = narrow(
        taps[0] * grad_wide + taps[1] * earlier(grad_wide, 1) + taps[2] * earlier(grad_wide, 2)
    )
    tap_terms = jnp.stack([jnp.sum(grad_wide * lag, axis=0) for lag in lags], axis=0)
    weight_terms = narrow(
        jnp.einsum("tr,tc->rc", embedded, grad_proj, preferred_element_type=jnp.float32)
    )
    mixer_part = mixer_out.reshape(peers, 2, chans, chans)
    tap_part = narrow(tap_terms).reshape(1, chans, -1)
    tap_part = jnp.broadcast_to(tap_part, (peers,) + tap_part.shape[1:])
    back = lax.all_to_all(
        jnp.concatenate(
            [weight_terms.reshape(peers, chans, -1), mixer_part[:, 0], mixer_part[:, 1], tap_part],
            axis=2,
        ),
        "tm",
        split_axis=0,
        concat_axis=0,
        tiled=True,
    )
    filter_grads = lag_grads(table, lag_re, lag_im, ends)
    mixer_rows, weight_grads = pl.pallas_call(
        unpack_kernel,
        out_shape=(
            jax.ShapeDtypeStruct((rows, width), jnp.bfloat16),
            jax.ShapeDtypeStruct((chans, 3 * width), jnp.float32),
        ),
        name="unpack",
    )(back)
    tap_grads = widen(
        back[:, :, 3 * chans + rows :].reshape(peers, 3, 3, chans).transpose(1, 2, 0, 3)
    ).reshape(3, 3 * width)
    return (mixer_rows, weight_grads, tap_grads, filter_grads)


def cis_tables(count_a, count_b, modulus):
    left = jnp.arange(count_a, dtype=jnp.int32)[:, None]
    right = jnp.arange(count_b, dtype=jnp.int32)[None, :]
    angle = 2.0 * math.pi / modulus * (left * right % modulus).astype(jnp.float32)
    return (jnp.cos(angle), jnp.sin(angle))


class Factored:
    def __init__(self, total):
        bits = total.bit_length() - 1
        first_len = 1 << (bits + 1) // 2
        second_len = total // first_len
        first_cos, first_sin = cis_tables(first_len, first_len // 2, first_len)
        second_cos, second_sin = cis_tables(second_len, second_len, second_len)
        self.total = total
        self.second_len = second_len
        self.twist_cos, self.twist_sin = cis_tables(first_len, second_len, total)
        self.first_both = jnp.concatenate([first_cos, -first_sin], axis=0)
        self.forward = jnp.block([[second_cos, -second_sin], [second_sin, second_cos]])
        self.inverse = jnp.block([[second_cos, second_sin], [-second_sin, second_cos]])

    def spectrum(self, series):
        series = widen(series)
        channels, length = series.shape
        rows_k = self.twist_cos.shape[0]
        half = self.first_both.shape[1]
        blocks = series.reshape(channels, half, length // half)
        part = jnp.einsum("ka,cab->ckb", self.first_both, blocks)
        part_re = part[:, :rows_k]
        part_im = part[:, rows_k:]
        turn_re = part_re * self.twist_cos + part_im * self.twist_sin
        turn_im = part_im * self.twist_cos - part_re * self.twist_sin
        turned = jnp.concatenate([turn_re, turn_im], axis=2)
        result = jnp.einsum("ckb,bm->ckm", turned, self.forward)
        return (result[:, :, : self.second_len], result[:, :, self.second_len :])

    def product(self, left, right, conjugate):
        left_re, left_im = left
        right_re, right_im = right
        if conjugate:
            right_im = -right_im
        return (left_re * right_re - left_im * right_im, left_re * right_im + left_im * right_re)

    def signal(self, pair):
        joined = jnp.concatenate(pair, axis=2)
        back = jnp.einsum("ckm,mb->ckb", joined, self.inverse)
        back_re = back[:, :, : self.second_len]
        back_im = back[:, :, self.second_len :]
        turn_re = back_re * self.twist_cos - back_im * self.twist_sin
        turn_im = back_im * self.twist_cos + back_re * self.twist_sin
        turned = jnp.concatenate([turn_re, turn_im], axis=1)
        blocks = jnp.einsum("ka,ckb->cab", self.first_both, turned)
        return blocks.reshape(joined.shape[0], -1) * (1.0 / self.total)


def delayed(array, steps):
    length = array.shape[1]
    return jnp.pad(array, ((0, 0), (steps, 0)))[:, :length]


def advanced(array, steps):
    return jnp.pad(array, ((0, 0), (0, steps)))[:, steps:]


def wide_local(token_ids, field_offsets, embed_table, w_in, short_taps, filters, cotangent):
    rows, width = cotangent.shape
    fields = token_ids.shape[1]
    peers = lax.axis_size("tm")
    me = lax.axis_index("tm")
    chans = width // peers
    length = rows * peers
    vocab = embed_table.shape[0]

    w_part = w_in.reshape(chans, 3, peers, chans).transpose(2, 0, 1, 3).reshape(peers, chans, 3 * chans)
    cot_part = cotangent.reshape(rows, peers, chans).transpose(1, 2, 0)
    tok_part = narrow(token_ids).T.reshape(1, chans, -1)
    tok_part = jnp.broadcast_to(tok_part, (peers,) + tok_part.shape[1:])
    sent = jnp.concatenate([w_part, cot_part, tok_part], axis=2)
    got = lax.all_to_all(sent, "tm", split_axis=0, concat_axis=0, tiled=True)
    w_own = got[:, :, : 3 * chans].reshape(width, 3 * chans)
    upstream = widen(got[:, :, 3 * chans : 3 * chans + rows].transpose(1, 0, 2).reshape(chans, length))
    tokens = got[:, :, 3 * chans + rows :].reshape(peers, fields, rows)
    tokens = tokens.transpose(1, 0, 2).reshape(fields, length).astype(jnp.int32)
    row_index = tokens + field_offsets[:, None]

    codes = lax.broadcasted_iota(jnp.int32, (vocab, length), 0)
    counts = jnp.zeros((vocab, length), jnp.float32)
    for field in range(fields):
        counts = counts + jnp.where(codes == row_index[field][None, :], 1.0, 0.0)
    embedded = narrow(
        jnp.einsum("vr,vt->rt", embed_table, narrow(counts), preferred_element_type=jnp.float32)
    )
    proj = narrow(jnp.einsum("rc,rt->ct", w_own, embedded, preferred_element_type=jnp.float32))
    taps = lax.dynamic_index_in_dim(short_taps.reshape(3, 3, peers, chans), me, 2, keepdims=False)
    taps = taps.reshape(3, 3 * chans, 1)
    proj_wide = widen(proj)
    lags = (proj_wide, delayed(proj_wide, 1), delayed(proj_wide, 2))
    mixed = narrow(taps[0] * lags[0] + taps[1] * lags[1] + taps[2] * lags[2])
    values = mixed[:chans]
    first_gate = widen(mixed[chans : 2 * chans])
    second_gate = widen(mixed[2 * chans :])

    transform = Factored(2 * length)

    def spectra(*series):
        whole = transform.spectrum(jnp.concatenate(series, axis=0))
        return [
            tuple(part[i * chans : (i + 1) * chans] for part in whole) for i in range(len(series))
        ]

    def signals(*pairs):
        whole = transform.signal(tuple(jnp.concatenate(parts, axis=0) for parts in zip(*pairs)))
        return [whole[i * chans : (i + 1) * chans] for i in range(len(pairs))]

    grad_conv2 = narrow(upstream * second_gate)
    first_spec, second_spec, value_spec, grad_spec2 = spectra(
        filters[0], filters[1], values, grad_conv2
    )
    first_conv, grad_mix = signals(
        transform.product(value_spec, first_spec, False),
        transform.product(grad_spec2, second_spec, True),
    )
    first_conv = widen(narrow(first_conv))
    grad_mix = widen(narrow(grad_mix))
    first_mix = narrow(first_gate * first_conv)
    grad_gate1 = narrow(grad_mix * first_conv)
    grad_conv1 = narrow(grad_mix * first_gate)
    mix_spec, grad_spec1 = spectra(first_mix, grad_conv1)
    second_conv, grad_values, filter_one, filter_two = signals(
        transform.product(mix_spec, second_spec, False),
        transform.product(grad_spec1, first_spec, True),
        transform.product(grad_spec1, value_spec, True),
        transform.product(grad_spec2, mix_spec, True),
    )
    second_conv = widen(narrow(second_conv))
    mixer_out = narrow(second_gate * second_conv)
    grad_gate2 = narrow(upstream * second_conv)
    filter_grads = jnp.stack([filter_one, filter_two], axis=0)
    grad_mixed = jnp.concatenate([narrow(grad_values), grad_gate1, grad_gate2], axis=0)
    grad_wide = widen(grad_mixed)
    grad_proj = narrow(
        taps[0] * grad_wide + taps[1] * advanced(grad_wide, 1) + taps[2] * advanced(grad_wide, 2)
    )
    tap_terms = jnp.stack([jnp.sum(grad_wide * lag, axis=1) for lag in lags], axis=0)
    weight_terms = narrow(
        jnp.einsum("rt,ct->rc", embedded, grad_proj, preferred_element_type=jnp.float32)
    )

    weight_part = weight_terms.reshape(peers, chans, 3 * chans)
    mixer_part = mixer_out.reshape(chans, peers, rows).transpose(1, 0, 2)
    tap_part = narrow(tap_terms).reshape(1, chans, -1)
    tap_part = jnp.broadcast_to(tap_part, (peers,) + tap_part.shape[1:])
    back = lax.all_to_all(
        jnp.concatenate([weight_part, mixer_part, tap_part], axis=2),
        "tm",
        split_axis=0,
        concat_axis=0,
        tiled=True,
    )
    weight_grads = widen(
        back[:, :, : 3 * chans].reshape(peers, chans, 3, chans).transpose(1, 2, 0, 3)
    ).reshape(chans, 3 * width)
    mixer_rows = back[:, :, 3 * chans : 3 * chans + rows].reshape(width, rows).T
    tap_grads = widen(
        back[:, :, 3 * chans + rows :].reshape(peers, 3, 3, chans).transpose(1, 2, 0, 3)
    ).reshape(3, 3 * width)
    return (mixer_rows, weight_grads, tap_grads, filter_grads)


def solution(mesh):
    return jax.shard_map(
        local,
        mesh=mesh,
        in_specs=(
            P(("groups", "tm"), None),
            P("groups"),
            P(),
            P("tm", None),
            P(),
            P(None, "tm", None),
            P(("groups", "tm"), None),
        ),
        out_specs=(
            P(("groups", "tm"), None),
            P(("groups", "tm"), None),
            P("groups", None),
            P("groups", "tm", None),
        ),
        check_vma=False,
    )
```

```python
import math

import jax
import jax.numpy as jnp
from jax import lax
from jax.experimental import pallas as pl
from jax.experimental.pallas import tpu as pltpu
from jax.sharding import PartitionSpec as P

DENSE_LIMIT = 4096
CODES = 128
CHUNK = 512
VMEM = 56 << 20


def widen(array):
    return array.astype(jnp.float32)


def narrow(array):
    return array.astype(jnp.bfloat16)


def dense_table(total):
    half = total // 2
    inner = 1 << (total.bit_length() - 1) // 2
    outer = half // inner
    step = lax.optimization_barrier(jnp.arange(half, dtype=jnp.int32))
    unit = 2.0 * math.pi / total

    def cis(count, stride):
        index = jnp.arange(count, dtype=jnp.int32)[:, None] * stride * step[None, :] % total
        angle = unit * index.astype(jnp.float32)
        return (jnp.cos(angle), jnp.sin(angle))

    coarse_cos, coarse_sin = cis(outer, inner)
    fine_cos, fine_sin = cis(inner, 1)
    whole = pl.BlockSpec(memory_space=pltpu.VMEM)
    return pl.pallas_call(
        table_kernel,
        grid=(outer,),
        out_shape=jax.ShapeDtypeStruct((2, half, half), jnp.bfloat16),
        in_specs=[whole] * 4,
        out_specs=pl.BlockSpec((2, inner, half), lambda i: (0, i, 0)),
        cost_estimate=pl.CostEstimate(
            flops=6 * half * half, bytes_accessed=4 * half * half, transcendentals=0
        ),
        compiler_params=pltpu.CompilerParams(vmem_limit_bytes=VMEM),
        name="table",
    )(coarse_cos, coarse_sin, fine_cos, fine_sin)


def table_kernel(coarse_cos, coarse_sin, fine_cos, fine_sin, out):
    row = pl.ds(pl.program_id(0), 1)
    high_cos, high_sin = coarse_cos[row, :], coarse_sin[row, :]
    low_cos, low_sin = fine_cos[...], fine_sin[...]
    out[0] = narrow(high_cos * low_cos - high_sin * low_sin)
    out[1] = narrow(-(high_sin * low_cos + high_cos * low_sin))


def embed_kernel(tokens, used, w_own, embedded, proj):
    picked = tokens[...]
    code = lax.broadcasted_iota(jnp.int32, (picked.shape[0], CODES), 1)
    chosen = [
        narrow(jnp.where(picked[:, field : field + 1] == code, 1.0, 0.0))
        for field in range(picked.shape[1])
    ]
    rows = narrow(
        jnp.dot(
            jnp.concatenate(chosen, axis=1), used[...], preferred_element_type=jnp.float32
        )
    )
    embedded[...] = rows
    proj[...] = narrow(jnp.dot(rows, w_own[...], preferred_element_type=jnp.float32))


def embed(tokens, used, w_own):
    length, fields = tokens.shape
    width, columns = w_own.shape
    block = 256
    whole = pl.BlockSpec(memory_space=pltpu.VMEM)
    return pl.pallas_call(
        embed_kernel,
        grid=(length // block,),
        out_shape=(
            jax.ShapeDtypeStruct((length, width), jnp.bfloat16),
            jax.ShapeDtypeStruct((length, columns), jnp.bfloat16),
        ),
        in_specs=[pl.BlockSpec((block, fields), lambda i: (i, 0)), whole, whole],
        out_specs=(
            pl.BlockSpec((block, width), lambda i: (i, 0)),
            pl.BlockSpec((block, columns), lambda i: (i, 0)),
        ),
        compiler_params=pltpu.CompilerParams(vmem_limit_bytes=24 << 20),
        name="embed",
    )(tokens, used, w_own)


def spread(rows, columns, start):
    row = lax.broadcasted_iota(jnp.int32, (rows, columns), 0) + start
    return 1.0 - 2.0 * (row & 1).astype(jnp.float32)


def dot(left, right):
    return jnp.dot(left, right, preferred_element_type=jnp.float32)


def quarter(rows, columns, start):
    turn = (lax.broadcasted_iota(jnp.int32, (rows, columns), 0) + start) & 3
    real = jnp.where(turn == 0, 1.0, jnp.where(turn == 2, -1.0, 0.0))
    imag = jnp.where(turn == 1, 1.0, jnp.where(turn == 3, -1.0, 0.0))
    return (real, imag)


def mixer_kernel(
    table_hbm, signals, gates, convs, gate_grad, lag_re, lag_im, ends, table, spec_re, spec_im, prod_re, prod_im, stage, sems
):
    half, pair = gates.shape
    middle = half // 2
    chans = pair // 2
    total = 2 * half
    chunk = min(CHUNK, middle)
    steps = half // chunk

    def window(step, base=0):
        return pl.ds(pl.multiple_of(step * chunk + base, chunk), chunk)

    def copy(part, step):
        rows = window(step)
        return pltpu.make_async_copy(
            table_hbm.at[part, rows], table.at[part, rows], sems.at[part, step]
        )

    for step in range(steps):
        copy(0, step).start()
        copy(1, step).start()

    parity = 1 - 2 * (lax.broadcasted_iota(jnp.int32, (16, half), 1) & 1)
    parity = parity.astype(jnp.float32).astype(jnp.bfloat16)
    early = lax.broadcasted_iota(jnp.int32, (1, pair), 1) < chans
    sign = jnp.where(early, 1.0, -1.0)

    def swap(value):
        return pltpu.roll(value, chans, 1)

    def keep(step, real, imag, to_re, to_im):
        rows = window(step)
        row = lax.broadcasted_iota(jnp.int32, (chunk, pair), 0) + step * chunk
        scale = jnp.where(row == 0, 1.0 / total, 2.0 / total)
        real, imag = real * scale, imag * scale
        cos, sin = quarter(chunk, pair, step * chunk)
        to_re[rows, :pair] = narrow(real)
        to_im[rows, :pair] = narrow(imag)
        to_re[rows, pair:] = narrow(cos * real - sin * imag)
        to_im[rows, pair:] = narrow(sin * real + cos * imag)

    alternating = dot(parity, signals[...])[:8]
    ends_filter = alternating[:, :pair]
    ends_value = alternating[:, pair:]

    def first(step, carry):
        rows = window(step)
        copy(0, step).wait()
        spec_re[rows, :] = dot(table[0, rows, :], signals[...])
        copy(1, step).wait()
        spec_im[rows, :] = dot(table[1, rows, :], signals[...])
        other_re, other_im = spec_re[rows, :pair], spec_im[rows, :pair]
        real, imag = spec_re[rows, pair:], spec_im[rows, pair:]
        keep(
            step,
            real * other_re - sign * imag * other_im,
            sign * real * other_im + imag * other_re,
            prod_re,
            prod_im,
        )
        return carry

    lax.fori_loop(0, steps, first, 0)
    ends_first = (ends_value * ends_filter * (1.0 / total))[:1]

    def second(step, carry):
        rows = window(step)
        both = dot(table[0, rows, :], prod_re[...]) + dot(table[1, rows, :], prod_im[...])
        weave = spread(chunk, pair, step * chunk) * ends_first
        for part in range(2):
            lanes = slice(part * pair, (part + 1) * pair)
            place = window(step, part * middle)
            out = widen(narrow(both[:, lanes] + weave))
            stage[rows, lanes] = narrow(out * widen(gates[place, :]))
            gate_grad[place, :] = narrow(out * swap(out))
        return carry

    lax.fori_loop(0, steps // 2, second, 0)
    ends_both = dot(parity[:, :middle], stage[...])[:8]
    ends_mix = ends_both[:, :pair] + ends_both[:, pair:]

    def third(step, carry):
        rows = window(step)
        half_re = dot(table[0, rows, :middle], stage[...])
        half_im = dot(table[1, rows, :middle], stage[...])
        cos, sin = quarter(chunk, pair, step * chunk)
        mixed_re = half_re[:, :pair] + cos * half_re[:, pair:] + sin * half_im[:, pair:]
        mixed_im = half_im[:, :pair] + cos * half_im[:, pair:] - sin * half_re[:, pair:]
        filt_re, filt_im = swap(spec_re[rows, :pair]), swap(spec_im[rows, :pair])
        flip_re, flip_im = swap(spec_re[rows, pair:]), swap(spec_im[rows, pair:])
        left_re = jnp.where(early, flip_re, mixed_re)
        left_im = jnp.where(early, flip_im, mixed_im)
        right_re = jnp.where(early, mixed_re, flip_re)
        right_im = jnp.where(early, mixed_im, flip_im)
        keep(
            step,
            mixed_re * filt_re - sign * mixed_im * filt_im,
            sign * mixed_re * filt_im + mixed_im * filt_re,
            prod_re,
            prod_im,
        )
        keep(
            step,
            left_re * right_re + left_im * right_im,
            left_im * right_re - left_re * right_im,
            lag_re,
            lag_im,
        )
        return carry

    lax.fori_loop(0, steps, third, 0)
    ends_conv = (ends_mix * swap(ends_filter) * (1.0 / total))[:1]
    ends[...] = ends_mix * swap(ends_value) * (1.0 / total)

    def fourth(step, carry):
        rows = window(step)
        both = dot(table[0, rows, :], prod_re[...]) + dot(table[1, rows, :], prod_im[...])
        weave = spread(chunk, pair, step * chunk) * ends_conv
        convs[rows, :] = narrow(both[:, :pair] + weave)
        convs[window(step, middle), :] = narrow(both[:, pair:] + weave)
        return carry

    lax.fori_loop(0, steps // 2, fourth, 0)


def lag_kernel(table_hbm, lag_re, lag_im, ends, filter_grads, table, sems):
    half, pair = lag_re.shape[0], lag_re.shape[1] // 2
    middle = half // 2
    chans = pair // 2
    chunk = min(CHUNK, middle)
    steps = middle // chunk

    def window(step, base=0):
        return pl.ds(pl.multiple_of(step * chunk + base, chunk), chunk)

    def copy(part, step):
        rows = window(step)
        return pltpu.make_async_copy(
            table_hbm.at[part, rows], table.at[part, rows], sems.at[part, step]
        )

    for step in range(steps):
        copy(0, step).start()
        copy(1, step).start()

    def body(step, carry):
        rows = window(step)
        copy(0, step).wait()
        copy(1, step).wait()
        both = dot(table[0, rows, :], lag_re[...]) + dot(table[1, rows, :], lag_im[...])
        weave = spread(chunk, pair, step * chunk) * ends[:1, :]
        for part in range(2):
            lagged = (both[:, part * pair : (part + 1) * pair] + weave).T
            place = window(step, part * middle)
            filter_grads[1, :, place] = lagged[:chans]
            filter_grads[0, :, place] = lagged[chans:]
        return carry

    lax.fori_loop(0, steps, body, 0)


def fused_mixer(table, signals, gates):
    half, pair = gates.shape
    steps = half // min(CHUNK, half // 2)
    whole = pl.BlockSpec(memory_space=pltpu.VMEM)
    wide = pltpu.VMEM((half, 2 * pair), jnp.float32)
    packed = pltpu.VMEM((half, 2 * pair), jnp.bfloat16)
    narrow_out = jax.ShapeDtypeStruct((half, pair), jnp.bfloat16)
    wide_out = jax.ShapeDtypeStruct((half, 2 * pair), jnp.bfloat16)
    return pl.pallas_call(
        mixer_kernel,
        out_shape=(
            narrow_out,
            narrow_out,
            wide_out,
            wide_out,
            jax.ShapeDtypeStruct((8, pair), jnp.float32),
        ),
        in_specs=[pl.BlockSpec(memory_space=pl.ANY), whole, whole],
        out_specs=(whole,) * 5,
        scratch_shapes=[
            pltpu.VMEM((2, half, half), jnp.bfloat16),
            wide,
            wide,
            packed,
            packed,
            pltpu.VMEM((half // 2, 2 * pair), jnp.bfloat16),
            pltpu.SemaphoreType.DMA((2, steps)),
        ],
        compiler_params=pltpu.CompilerParams(vmem_limit_bytes=VMEM),
        cost_estimate=pl.CostEstimate(
            flops=20 * half * half * pair, bytes_accessed=4 * half * half, transcendentals=0
        ),
        name="mixer",
    )(table, signals, gates)


def lag_grads(table, lag_re, lag_im, ends):
    half, pair = lag_re.shape[0], lag_re.shape[1] // 2
    middle = half // 2
    steps = middle // min(CHUNK, middle)
    whole = pl.BlockSpec(memory_space=pltpu.VMEM)
    return pl.pallas_call(
        lag_kernel,
        out_shape=jax.ShapeDtypeStruct((2, pair // 2, half), jnp.float32),
        in_specs=[pl.BlockSpec(memory_space=pl.ANY), whole, whole, whole],
        out_specs=whole,
        scratch_shapes=[
            pltpu.VMEM((2, middle, half), jnp.bfloat16),
            pltpu.SemaphoreType.DMA((2, steps)),
        ],
        compiler_params=pltpu.CompilerParams(vmem_limit_bytes=24 << 20),
        cost_estimate=pl.CostEstimate(
            flops=4 * half * half * pair, bytes_accessed=3 * half * half, transcendentals=0
        ),
        name="lags",
    )(table, lag_re, lag_im, ends)


def pack_kernel(w_ref, cot_ref, tok_ref, out_ref):
    peers, chans, _ = out_ref.shape
    rows, width = cot_ref.shape
    tok = tok_ref[...]
    for peer in range(peers):
        own = slice(peer * chans, (peer + 1) * chans)
        pieces = [w_ref[:, j * width + peer * chans : j * width + (peer + 1) * chans] for j in range(3)]
        pieces += [cot_ref[:chans, own], cot_ref[chans:, own], tok[:chans], tok[chans:]]
        out_ref[peer] = jnp.concatenate(pieces, axis=1)


def unpack_kernel(got_ref, mixer_ref, weight_ref):
    peers, chans, _ = got_ref.shape
    width = peers * chans
    for peer in range(0, peers, 2):
        low, high = got_ref[peer], got_ref[peer + 1]
        for j in range(5):
            own = slice(j * chans, (j + 1) * chans)
            both = jnp.concatenate([low[:, own], high[:, own]], axis=1)
            if j < 3:
                start = j * width + peer * chans
                weight_ref[:, start : start + 2 * chans] = widen(both)
            else:
                top = (j - 3) * chans
                mixer_ref[top : top + chans, peer * chans : (peer + 2) * chans] = both


def local(token_ids, field_offsets, embed_table, w_in, short_taps, filters, cotangent):
    chans = cotangent.shape[1] // lax.axis_size("tm")
    dense = 2 * cotangent.shape[0] * lax.axis_size("tm") <= DENSE_LIMIT
    plan = fast_local if dense and chans == 64 and cotangent.shape[0] == 2 * chans else wide_local
    return plan(token_ids, field_offsets, embed_table, w_in, short_taps, filters, cotangent)


def later(array, steps):
    return jnp.pad(array, ((steps, 0), (0, 0)))[: array.shape[0]]


def earlier(array, steps):
    return jnp.pad(array, ((0, steps), (0, 0)))[steps:]


def fast_local(token_ids, field_offsets, embed_table, w_in, short_taps, filters, cotangent):
    rows, width = cotangent.shape
    fields = token_ids.shape[1]
    peers = lax.axis_size("tm")
    me = lax.axis_index("tm")
    chans = width // peers
    length = rows * peers
    lanes = 3 * chans + rows + 2 * fields
    sent = pl.pallas_call(
        pack_kernel,
        out_shape=jax.ShapeDtypeStruct((peers, chans, lanes), jnp.bfloat16),
        name="pack",
    )(w_in, cotangent, narrow(token_ids))
    got = lax.all_to_all(sent, "tm", split_axis=0, concat_axis=0, tiled=True)
    table = dense_table(2 * length)
    used_rows = field_offsets[:, None] + jnp.arange(CODES, dtype=jnp.int32)[None, :]
    used = jnp.take(embed_table, used_rows.reshape(-1), axis=0, mode="clip")
    filter_rows = filters.transpose(2, 0, 1).reshape(length, 2 * chans)

    def halves(start, count):
        first = got[:, :, start : start + count]
        second = got[:, :, start + count : start + 2 * count]
        return jnp.concatenate([first, second], axis=1).reshape(length, count)

    w_own = got[:, :, : 3 * chans].reshape(width, 3 * chans)
    upstream = widen(halves(3 * chans, chans))
    tokens = halves(3 * chans + rows, fields).astype(jnp.int32)
    embedded, proj = embed(tokens, used, w_own)
    taps = lax.dynamic_index_in_dim(short_taps.reshape(3, 3, peers, chans), me, 2, keepdims=False)
    taps = taps.reshape(3, 1, 3 * chans)
    proj_wide = widen(proj)
    lags = (proj_wide, later(proj_wide, 1), later(proj_wide, 2))
    mixed = narrow(taps[0] * lags[0] + taps[1] * lags[1] + taps[2] * lags[2])
    values = mixed[:, :chans]
    first_gate = mixed[:, chans : 2 * chans]
    second_gate = widen(mixed[:, 2 * chans :])
    grad_conv2 = narrow(upstream * second_gate)
    convs, gate_grad, lag_re, lag_im, ends = fused_mixer(
        table,
        jnp.concatenate([filter_rows, values, grad_conv2], axis=1),
        jnp.concatenate([first_gate, first_gate], axis=1),
    )
    second_conv = widen(convs[:, :chans])
    mixer_out = narrow(second_gate * second_conv)
    grad_gate2 = narrow(upstream * second_conv)
    grad_mixed = jnp.concatenate([convs[:, chans:], gate_grad[:, :chans], grad_gate2], axis=1)
    grad_wide = widen(grad_mixed)
    grad_proj = narrow(
        taps[0] * grad_wide + taps[1] * earlier(grad_wide, 1) + taps[2] * earlier(grad_wide, 2)
    )
    tap_terms = jnp.stack([jnp.sum(grad_wide * lag, axis=0) for lag in lags], axis=0)
    weight_terms = narrow(
        jnp.einsum("tr,tc->rc", embedded, grad_proj, preferred_element_type=jnp.float32)
    )
    mixer_part = mixer_out.reshape(peers, 2, chans, chans)
    tap_part = narrow(tap_terms).reshape(1, chans, -1)
    tap_part = jnp.broadcast_to(tap_part, (peers,) + tap_part.shape[1:])
    back = lax.all_to_all(
        jnp.concatenate(
            [weight_terms.reshape(peers, chans, -1), mixer_part[:, 0], mixer_part[:, 1], tap_part],
            axis=2,
        ),
        "tm",
        split_axis=0,
        concat_axis=0,
        tiled=True,
    )
    filter_grads = lag_grads(table, lag_re, lag_im, ends)
    mixer_rows, weight_grads = pl.pallas_call(
        unpack_kernel,
        out_shape=(
            jax.ShapeDtypeStruct((rows, width), jnp.bfloat16),
            jax.ShapeDtypeStruct((chans, 3 * width), jnp.float32),
        ),
        name="unpack",
    )(back)
    tap_grads = widen(
        back[:, :, 3 * chans + rows :].reshape(peers, 3, 3, chans).transpose(1, 2, 0, 3)
    ).reshape(3, 3 * width)
    return (mixer_rows, weight_grads, tap_grads, filter_grads)


def cis_tables(count_a, count_b, modulus):
    left = jnp.arange(count_a, dtype=jnp.int32)[:, None]
    right = jnp.arange(count_b, dtype=jnp.int32)[None, :]
    angle = 2.0 * math.pi / modulus * (left * right % modulus).astype(jnp.float32)
    return (jnp.cos(angle), jnp.sin(angle))


class Factored:
    def __init__(self, total):
        bits = total.bit_length() - 1
        first_len = 1 << (bits + 1) // 2
        second_len = total // first_len
        first_cos, first_sin = cis_tables(first_len, first_len // 2, first_len)
        second_cos, second_sin = cis_tables(second_len, second_len, second_len)
        self.total = total
        self.second_len = second_len
        self.twist_cos, self.twist_sin = cis_tables(first_len, second_len, total)
        self.first_both = jnp.concatenate([first_cos, -first_sin], axis=0)
        self.forward = jnp.block([[second_cos, -second_sin], [second_sin, second_cos]])
        self.inverse = jnp.block([[second_cos, second_sin], [-second_sin, second_cos]])

    def spectrum(self, series):
        series = widen(series)
        channels, length = series.shape
        rows_k = self.twist_cos.shape[0]
        half = self.first_both.shape[1]
        blocks = series.reshape(channels, half, length // half)
        part = jnp.einsum("ka,cab->ckb", self.first_both, blocks)
        part_re = part[:, :rows_k]
        part_im = part[:, rows_k:]
        turn_re = part_re * self.twist_cos + part_im * self.twist_sin
        turn_im = part_im * self.twist_cos - part_re * self.twist_sin
        turned = jnp.concatenate([turn_re, turn_im], axis=2)
        result = jnp.einsum("ckb,bm->ckm", turned, self.forward)
        return (result[:, :, : self.second_len], result[:, :, self.second_len :])

    def product(self, left, right, conjugate):
        left_re, left_im = left
        right_re, right_im = right
        if conjugate:
            right_im = -right_im
        return (left_re * right_re - left_im * right_im, left_re * right_im + left_im * right_re)

    def signal(self, pair):
        joined = jnp.concatenate(pair, axis=2)
        back = jnp.einsum("ckm,mb->ckb", joined, self.inverse)
        back_re = back[:, :, : self.second_len]
        back_im = back[:, :, self.second_len :]
        turn_re = back_re * self.twist_cos - back_im * self.twist_sin
        turn_im = back_im * self.twist_cos + back_re * self.twist_sin
        turned = jnp.concatenate([turn_re, turn_im], axis=1)
        blocks = jnp.einsum("ka,ckb->cab", self.first_both, turned)
        return blocks.reshape(joined.shape[0], -1) * (1.0 / self.total)


def delayed(array, steps):
    length = array.shape[1]
    return jnp.pad(array, ((0, 0), (steps, 0)))[:, :length]


def advanced(array, steps):
    return jnp.pad(array, ((0, 0), (0, steps)))[:, steps:]


def wide_local(token_ids, field_offsets, embed_table, w_in, short_taps, filters, cotangent):
    rows, width = cotangent.shape
    fields = token_ids.shape[1]
    peers = lax.axis_size("tm")
    me = lax.axis_index("tm")
    chans = width // peers
    length = rows * peers
    vocab = embed_table.shape[0]

    w_part = w_in.reshape(chans, 3, peers, chans).transpose(2, 0, 1, 3).reshape(peers, chans, 3 * chans)
    cot_part = cotangent.reshape(rows, peers, chans).transpose(1, 2, 0)
    tok_part = narrow(token_ids).T.reshape(1, chans, -1)
    tok_part = jnp.broadcast_to(tok_part, (peers,) + tok_part.shape[1:])
    sent = jnp.concatenate([w_part, cot_part, tok_part], axis=2)
    got = lax.all_to_all(sent, "tm", split_axis=0, concat_axis=0, tiled=True)
    w_own = got[:, :, : 3 * chans].reshape(width, 3 * chans)
    upstream = widen(got[:, :, 3 * chans : 3 * chans + rows].transpose(1, 0, 2).reshape(chans, length))
    tokens = got[:, :, 3 * chans + rows :].reshape(peers, fields, rows)
    tokens = tokens.transpose(1, 0, 2).reshape(fields, length).astype(jnp.int32)
    row_index = tokens + field_offsets[:, None]

    codes = lax.broadcasted_iota(jnp.int32, (vocab, length), 0)
    counts = jnp.zeros((vocab, length), jnp.float32)
    for field in range(fields):
        counts = counts + jnp.where(codes == row_index[field][None, :], 1.0, 0.0)
    embedded = narrow(
        jnp.einsum("vr,vt->rt", embed_table, narrow(counts), preferred_element_type=jnp.float32)
    )
    proj = narrow(jnp.einsum("rc,rt->ct", w_own, embedded, preferred_element_type=jnp.float32))
    taps = lax.dynamic_index_in_dim(short_taps.reshape(3, 3, peers, chans), me, 2, keepdims=False)
    taps = taps.reshape(3, 3 * chans, 1)
    proj_wide = widen(proj)
    lags = (proj_wide, delayed(proj_wide, 1), delayed(proj_wide, 2))
    mixed = narrow(taps[0] * lags[0] + taps[1] * lags[1] + taps[2] * lags[2])
    values = mixed[:chans]
    first_gate = widen(mixed[chans : 2 * chans])
    second_gate = widen(mixed[2 * chans :])

    transform = Factored(2 * length)

    def spectra(*series):
        whole = transform.spectrum(jnp.concatenate(series, axis=0))
        return [
            tuple(part[i * chans : (i + 1) * chans] for part in whole) for i in range(len(series))
        ]

    def signals(*pairs):
        whole = transform.signal(tuple(jnp.concatenate(parts, axis=0) for parts in zip(*pairs)))
        return [whole[i * chans : (i + 1) * chans] for i in range(len(pairs))]

    grad_conv2 = narrow(upstream * second_gate)
    first_spec, second_spec, value_spec, grad_spec2 = spectra(
        filters[0], filters[1], values, grad_conv2
    )
    first_conv, grad_mix = signals(
        transform.product(value_spec, first_spec, False),
        transform.product(grad_spec2, second_spec, True),
    )
    first_conv = widen(narrow(first_conv))
    grad_mix = widen(narrow(grad_mix))
    first_mix = narrow(first_gate * first_conv)
    grad_gate1 = narrow(grad_mix * first_conv)
    grad_conv1 = narrow(grad_mix * first_gate)
    mix_spec, grad_spec1 = spectra(first_mix, grad_conv1)
    second_conv, grad_values, filter_one, filter_two = signals(
        transform.product(mix_spec, second_spec, False),
        transform.product(grad_spec1, first_spec, True),
        transform.product(grad_spec1, value_spec, True),
        transform.product(grad_spec2, mix_spec, True),
    )
    second_conv = widen(narrow(second_conv))
    mixer_out = narrow(second_gate * second_conv)
    grad_gate2 = narrow(upstream * second_conv)
    filter_grads = jnp.stack([filter_one, filter_two], axis=0)
    grad_mixed = jnp.concatenate([narrow(grad_values), grad_gate1, grad_gate2], axis=0)
    grad_wide = widen(grad_mixed)
    grad_proj = narrow(
        taps[0] * grad_wide + taps[1] * advanced(grad_wide, 1) + taps[2] * advanced(grad_wide, 2)
    )
    tap_terms = jnp.stack([jnp.sum(grad_wide * lag, axis=1) for lag in lags], axis=0)
    weight_terms = narrow(
        jnp.einsum("rt,ct->rc", embedded, grad_proj, preferred_element_type=jnp.float32)
    )

    weight_part = weight_terms.reshape(peers, chans, 3 * chans)
    mixer_part = mixer_out.reshape(chans, peers, rows).transpose(1, 0, 2)
    tap_part = narrow(tap_terms).reshape(1, chans, -1)
    tap_part = jnp.broadcast_to(tap_part, (peers,) + tap_part.shape[1:])
    back = lax.all_to_all(
        jnp.concatenate([weight_part, mixer_part, tap_part], axis=2),
        "tm",
        split_axis=0,
        concat_axis=0,
        tiled=True,
    )
    weight_grads = widen(
        back[:, :, : 3 * chans].reshape(peers, chans, 3, chans).transpose(1, 2, 0, 3)
    ).reshape(chans, 3 * width)
    mixer_rows = back[:, :, 3 * chans : 3 * chans + rows].reshape(width, rows).T
    tap_grads = widen(
        back[:, :, 3 * chans + rows :].reshape(peers, 3, 3, chans).transpose(1, 2, 0, 3)
    ).reshape(3, 3 * width)
    return (mixer_rows, weight_grads, tap_grads, filter_grads)


def solution(mesh):
    return jax.shard_map(
        local,
        mesh=mesh,
        in_specs=(
            P(("groups", "tm"), None),
            P("groups"),
            P(),
            P("tm", None),
            P(),
            P(None, "tm", None),
            P(("groups", "tm"), None),
        ),
        out_specs=(
            P(("groups", "tm"), None),
            P(("groups", "tm"), None),
            P("groups", None),
            P("groups", "tm", None),
        ),
        check_vma=False,
    )
```
